32 devices in a mesh: wide: 16 (over z, x, core), narrow: 2 (over y).
Axes of the slice: x: 2, y: 2, z: 4, core: 2. Of those that a mesh axis runs over, the one named last changes fastest.
Arguments:
- hidden: bfloat16 [128, 16384], P('wide', 'narrow'), may hold values from -6 to 6
- down_weight: bfloat16 [16384, 4096], P(('wide', 'narrow')), may hold values from -0.046875 to 0.046875
- rotation: float32 [4096, 4096], P('wide', 'narrow'), may hold values from -1 to 1, as said below
- cotangent: bfloat16 [128, 4096], P('wide', 'narrow'), may hold values from -6 to 6
- token_exps: int32 [128], P('wide'), may hold values from -2 to 0
- column_exps: int32 [4096], P('narrow'), may hold values from -9 to -7
- sign_bits: int32 [16384], P('narrow'), may hold values 0 or 1
- step_size: float32 [], replicated, may hold values from 0.00015 to 0.0003
Outputs:
- projected: bfloat16 [128, 4096], P('wide', 'narrow')
- new_rotation: float32 [4096, 4096], P('wide', 'narrow')
The draws below stay inside these ranges and needn't reach their ends.
Inputs may be any that keep to these rules, and one draw needn't show every extreme that they name: `rotation`: an orthogonal matrix up to float32 rounding.
All inputs are finite; a program needn't handle non-finite values. No bound on the sum of `sign_bits` on one device may be relied on, other than what follows from the above.
Results may differ from the reference program's by a relative error of at most 0.003.
The reference program's roundings to bfloat16 on the way (of `quantized`, `weight_quant` and `unrotated`) count: a program that leaves them out, or rounds other values in their place, can miss the bound.
Values may be sent and summed in bfloat16 or wider, within the bound.
No kernel may reach another device: no remote copies, remote signals or barrier semaphores. Data moves between devices by JAX's collectives and lax.ppermute only.
A program may use at most 128 MiB of HBM per device.

```python
import math
import jax
import jax.numpy as jnp
from jax import lax

D = 4096
FF = 16384
TOKENS = 128
ITERS = 1


def draw_rotation(key, part):
    base = jax.random.normal(key, (D, D), jnp.float32)
    factor_q, factor_r = jnp.linalg.qr(base)
    return factor_q.astype(jnp.float32)


def set_ends(drawn, key, least, largest):
    dims = drawn.shape
    place = [jax.random.randint(jax.random.fold_in(key, axis), (), 0, dims[axis]) for axis in range(len(dims))]
    drawn = drawn.at[tuple(place)].set(least)
    longest = dims.index(max(dims))
    place[longest] = (place[longest] + 1) % dims[longest]
    return drawn.at[tuple(place)].set(largest)


def steps_of(stream_key, shape, cuts, smallest, high):
    loudness = 1.0
    for dim, shards_of in cuts:
        draws = jax.random.uniform(jax.random.fold_in(jax.random.fold_in(stream_key, 6), dim), (shards_of,), jnp.float32, smallest / len(cuts), high / len(cuts))
        loudness = loudness * jnp.repeat(jnp.exp(draws), shape[dim] // shards_of).reshape((-1,) + (1,) * (len(shape) - 1 - dim))
    return loudness


def centred(stream_key, dims, width, bound, shards=(), kind=jnp.bfloat16):
    loudness = steps_of(stream_key, dims, shards, -0.22, 0.18) if shards else 1.0
    entries = jax.random.normal(stream_key, dims, jnp.float32) * width * loudness
    return jnp.minimum(jnp.maximum(entries, -bound), bound).astype(kind)


def setup_inputs(seed: int = 0) -> dict:
    keys = jax.random.split(jax.random.key(seed), 9)
    hidden = centred(keys[0], (TOKENS, FF), 1.0, 6.0, ((0, 16), (1, 2)))
    down_weight = centred(keys[1], (FF, D), FF ** -0.5, 0.046875, ((0, 32),))
    rotation = draw_rotation(jax.random.fold_in(keys[8], 71), 0)
    cotangent = centred(keys[3], (TOKENS, D), 1.0, 6.0, ((0, 16), (1, 2)))
    token_exps = set_ends(jax.random.randint(keys[4], (TOKENS,), -2, 1), jax.random.fold_in(keys[4], 1), -2, 0).astype(jnp.int32)
    column_exps = set_ends(jax.random.randint(keys[5], (D,), -9, -6), jax.random.fold_in(keys[5], 1), -9, (-6) - 1).astype(jnp.int32)
    sign_bits = set_ends((jax.random.randint(keys[6], (FF,), 0, 2) < 1).astype(jnp.int32), jax.random.fold_in(keys[6], 1), 0, 1)
    step_size = jnp.clip(jnp.exp(jax.random.uniform(keys[7], (), jnp.float32, math.log(0.00015), math.log(0.0003))), 0.00015, 0.0003)
    return {"hidden": hidden, "down_weight": down_weight, "rotation": rotation, "cotangent": cotangent, "token_exps": token_exps, "column_exps": column_exps, "sign_bits": sign_bits, "step_size": step_size}


HIGHEST_PREC = lax.Precision.HIGHEST
LEVELS = 7.0
TWO_PI = 2.0 * math.pi

def sylvester(length):
    positions = jnp.arange(length, dtype=jnp.int32)
    common = jnp.bitwise_and(positions[:, None], positions[None, :])
    parity = jnp.zeros((length, length), jnp.int32)
    for offset in range(max(length.bit_length() - 1, 0)):
        parity = parity + jnp.bitwise_and(jnp.right_shift(common, offset), 1)
    return (1 - 2 * (parity % 2)).astype(jnp.float32)

def local_hadamard(values):
    row_count, length = values.shape
    inner_size = min(length, 128)
    outer_size = length // inner_size
    blocks = values.reshape(row_count, outer_size, inner_size)
    blocks = jnp.einsum('rab,bc->rac', blocks, sylvester(inner_size), precision=HIGHEST_PREC)
    blocks = jnp.einsum('rab,ac->rcb', blocks, sylvester(outer_size), precision=HIGHEST_PREC)
    return blocks.reshape(row_count, length)

def fake_quant(values, exponents):
    scales = jnp.exp2(exponents.astype(jnp.float32))
    clipped = LEVELS * jnp.tanh(values / scales / LEVELS)
    return scales * (clipped - jnp.sin(TWO_PI * clipped) / TWO_PI)

def reference(hidden, down_weight, rotation, cotangent, token_exps, column_exps, sign_bits, step_size):
    sign_flip = (1 - 2 * sign_bits).astype(jnp.float32)
    mixed_in = hidden.astype(jnp.float32) * sign_flip[None, :]
    rotated = local_hadamard(mixed_in) / math.sqrt(FF)
    quantized = fake_quant(rotated, token_exps[:, None]).astype(jnp.bfloat16)
    weight_rot = jnp.dot(down_weight.astype(jnp.float32), rotation.astype(jnp.bfloat16).astype(jnp.float32), preferred_element_type=jnp.float32)
    weight_quant = fake_quant(weight_rot, column_exps[None, :]).astype(jnp.bfloat16)
    projected = jnp.dot(quantized.astype(jnp.float32), weight_quant.astype(jnp.float32), preferred_element_type=jnp.float32).astype(jnp.bfloat16)
    unrotated = jnp.dot(quantized.astype(jnp.float32), down_weight.astype(jnp.float32), preferred_element_type=jnp.float32).astype(jnp.bfloat16)
    gradient = jnp.dot(unrotated.T.astype(jnp.float32), cotangent.astype(jnp.float32), preferred_element_type=jnp.float32)
    product = jnp.dot(gradient, rotation.T, precision=HIGHEST_PREC)
    skew_part = product - product.T
    current = rotation - step_size * gradient
    for repeat in range(ITERS):
        current = rotation - 0.5 * step_size * jnp.dot(skew_part, rotation + current, precision=HIGHEST_PREC)
    return (projected, math.sqrt(D) * current)
```

```python
import functools
import math

import jax
import jax.numpy as jnp
import numpy as np
from jax import lax
from jax.experimental import pallas as pl
from jax.experimental.pallas import tpu as pltpu
from jax.sharding import PartitionSpec as P


LEVELS = 7.0
TWO_PI = 2.0 * math.pi
SINE = [(-1.0) ** k * TWO_PI ** (2 * k) / math.factorial(2 * k + 1) for k in range(1, 9)]
VMEM_LIMIT = 60 * 2**20


def fake_quant(values, inverse, scales):
    clipped = LEVELS * jnp.tanh(values * inverse)
    rest = clipped - jnp.floor(clipped + 0.5)
    square = rest * rest
    series = jnp.full_like(rest, SINE[-1])
    for term in SINE[-2::-1]:
        series = series * square + term
    return scales * (clipped - (rest + rest * square * series))


def parity_signs(length):
    row = lax.broadcasted_iota(jnp.int32, (length, length), 0)
    col = lax.broadcasted_iota(jnp.int32, (length, length), 1)
    common = row & col
    parity = jnp.zeros_like(common)
    for offset in range(length.bit_length() - 1):
        parity = parity ^ ((common >> offset) & 1)
    return (1 - 2 * parity).astype(jnp.float32).astype(jnp.bfloat16)


def split3(values):
    high = values.astype(jnp.bfloat16)
    rest = values - high.astype(jnp.float32)
    mid = rest.astype(jnp.bfloat16)
    low = (rest - mid.astype(jnp.float32)).astype(jnp.bfloat16)
    return high, mid, low


def hadamard_kernel(outer, x_ref, scale_ref, inverse_ref, out_ref):
    inner = x_ref.shape[1]
    mixed = jnp.dot(x_ref[...], parity_signs(inner), preferred_element_type=jnp.float32)
    signs = parity_signs(outer)
    for row in range(x_ref.shape[0] // outer):
        block = slice(row * outer, (row + 1) * outer)
        total = jnp.zeros((outer, inner), jnp.float32)
        for part in split3(mixed[block]):
            total = total + jnp.dot(signs, part, preferred_element_type=jnp.float32)
        total = total * (1.0 / math.sqrt(outer * inner))
        out_ref[block, :] = fake_quant(total, inverse_ref[block, :], scale_ref[block, :]).astype(out_ref.dtype)


def quantized_tokens(flipped, token_exps):
    rows, length = flipped.shape
    inner = min(length, 128)
    outer = length // inner
    scale = jnp.exp2(token_exps.astype(jnp.float32))
    spread = lambda v: jnp.broadcast_to(v[:, None, None], (rows, outer, 1)).reshape(rows * outer, 1)
    out = pl.pallas_call(
        functools.partial(hadamard_kernel, outer),
        out_shape=jax.ShapeDtypeStruct((rows * outer, inner), jnp.bfloat16),
        compiler_params=pltpu.CompilerParams(vmem_limit_bytes=16 * 2**20),
        cost_estimate=pl.CostEstimate(flops=8 * rows * length * 128, bytes_accessed=4 * rows * length, transcendentals=rows * length),
    )(flipped.reshape(rows * outer, inner), spread(scale), spread(1.0 / (LEVELS * scale)))
    return out.reshape(rows, length)


def panel_kernel(shape, order_ref, q_ref, u_ref, inverse_ref, scale_ref, *refs):
    parts, per_part, w_count, tile, depth, with_mix = shape
    w_refs, refs = refs[:w_count], refs[w_count:]
    blocks, refs = refs[: parts * per_part], refs[parts * per_part :]
    if with_mix:
        out_ref, mix_ref, w_v, r_v, w_sem, r_sem = refs
    else:
        out_ref, w_v, r_v, w_sem, r_sem = refs
    step = pl.program_id(0)
    steps = pl.num_programs(0)
    part_steps = steps // parts

    def w_copies():
        start, out = 0, []
        for k, ref in enumerate(w_refs):
            rows = ref.shape[0]
            out.append(pltpu.make_async_copy(ref, w_v.at[pl.ds(start, rows), :], w_sem.at[k]))
            start += rows
        return out

    def r_copies(part, inside, slot):
        cols = pl.ds(pl.multiple_of(inside * tile, tile), tile)
        return [
            pltpu.make_async_copy(
                blocks[part * per_part + k].at[pl.ds(0, depth), cols],
                r_v.at[slot, pl.ds(pl.multiple_of(order_ref[k] * depth, depth), depth), :],
                r_sem.at[slot, k],
            )
            for k in range(per_part)
        ]

    def start_tile(at, slot):
        for part in range(parts):

            @pl.when(lax.div(at, part_steps) == part)
            def _():
                for copy in r_copies(part, at - part * part_steps, slot):
                    copy.start()

    slot = lax.rem(step, 2)

    @pl.when(step == 0)
    def _():
        for copy in r_copies(0, 0, 0):
            copy.start()
        for copy in w_copies():
            copy.start()

    @pl.when(step + 1 < steps)
    def _():
        start_tile(step + 1, 1 - slot)

    for copy in r_copies(0, 0, slot):
        copy.wait()
    tile_r = r_v.at[slot]
    if with_mix:
        mix_ref[...] = jnp.dot(u_ref[...], tile_r[...], preferred_element_type=jnp.float32)

    @pl.when(step == 0)
    def _():
        for copy in w_copies():
            copy.wait()

    total = jnp.zeros(out_ref.shape, jnp.float32)
    height = w_v.shape[0]
    piece = min(height, 512)
    for at in range(0, height, piece):
        turned = jnp.dot(w_v[at : at + piece, :], tile_r[...], preferred_element_type=jnp.float32)
        coded = fake_quant(turned, inverse_ref[...], scale_ref[...]).astype(jnp.bfloat16)
        total = total + jnp.dot(q_ref[:, at : at + piece], coded, preferred_element_type=jnp.float32)
    out_ref[...] = total


def panel_product(order, q, u_full, inverse, scale, w_parts, block_parts, with_mix):
    tokens, height = q.shape
    width = w_parts[0].shape[1]
    parts, per_part = len(block_parts), len(block_parts[0])
    depth = width // per_part
    part_cols = block_parts[0][0].shape[1]
    cols = parts * part_cols
    tile = min(part_cols, 512)
    whole = lambda a: pl.BlockSpec(a.shape, lambda j, o: (0, 0), pipeline_mode=pl.Buffered(1))
    col_tile = lambda rows: pl.BlockSpec((rows, tile), lambda j, o: (0, j))
    flat = [b for part in block_parts for b in part]
    outs = [jax.ShapeDtypeStruct((tokens, cols), jnp.float32)] * (2 if with_mix else 1)
    shape = (parts, per_part, len(w_parts), tile, depth, with_mix)
    u_in = u_full if with_mix else q
    flops = 2 * cols * (height * width + tokens * height + (tokens * width if with_mix else 0))
    return pl.pallas_call(
        functools.partial(panel_kernel, shape),
        grid_spec=pltpu.PrefetchScalarGridSpec(
            num_scalar_prefetch=1,
            grid=(cols // tile,),
            in_specs=[whole(q), whole(u_in), col_tile(1), col_tile(1)]
            + [pl.BlockSpec(memory_space=pl.ANY)] * (len(w_parts) + len(flat)),
            out_specs=[col_tile(tokens)] * len(outs),
            scratch_shapes=[
                pltpu.VMEM((height, width), jnp.bfloat16),
                pltpu.VMEM((2, width, tile), jnp.bfloat16),
                pltpu.SemaphoreType.DMA((len(w_parts),)),
                pltpu.SemaphoreType.DMA((2, per_part)),
            ],
        ),
        out_shape=outs,
        compiler_params=pltpu.CompilerParams(vmem_limit_bytes=VMEM_LIMIT),
        cost_estimate=pl.CostEstimate(flops=flops, bytes_accessed=2 * width * (cols + height), transcendentals=cols * height),
    )(order, q, u_in, inverse, scale, *w_parts, *flat)


def ladder_ring(chips):
    return list(range(0, chips, 2)) + list(range(chips - 1 - chips % 2, 0, -2))


def on_device(wide, narrow, hidden, down_weight, rotation, cotangent, token_exps, column_exps, sign_bits, step_size):
    chips = wide // 2
    paired = narrow == 2 and wide % 2 == 0 and 2 <= chips <= 8
    place_wide = lax.axis_index("wide")
    place_narrow = lax.axis_index("narrow")
    core = place_wide % 2
    siblings = [(w, w ^ 1) for w in range(wide)]
    same_core = [[2 * c + side for c in range(chips)] for side in range(2)]
    swap = [(0, 1), (1, 0)]
    other_narrow = lambda a: lax.ppermute(a, "narrow", swap)
    other_core = lambda a: lax.ppermute(a, "wide", siblings)

    def sum_narrow(a):
        return a + other_narrow(a) if paired else lax.psum(a, "narrow")

    def exchange(a):
        return lax.all_to_all(a, "wide", 0, 0, axis_index_groups=same_core, tiled=True)

    def scatter_chips(pieces):
        sent = other_core(lax.dynamic_index_in_dim(pieces, 1 - core, 1, keepdims=False))
        kept = lax.dynamic_index_in_dim(pieces, core, 1, keepdims=False)
        return jnp.sum(exchange(kept + sent), axis=0)

    flip = (1 - 2 * sign_bits).astype(jnp.bfloat16)
    flipped = hidden * flip[None, :]
    block_rows, col_width = rotation.shape
    rot_half = rotation.astype(jnp.bfloat16)
    tokens = cotangent.shape[0] * wide
    units, width = down_weight.shape

    if paired:
        far = other_narrow(flipped)
        first = jnp.where(place_narrow == 0, flipped, far)
        second = jnp.where(place_narrow == 0, far, flipped)
        joined = jnp.concatenate([first, second], axis=1)
    else:
        joined = lax.all_gather(flipped, "narrow", axis=1, tiled=True)
    token_block = quantized_tokens(joined, token_exps)
    quantized = lax.all_to_all(token_block, "wide", split_axis=1, concat_axis=0, tiled=True)
    q_own = lax.dynamic_slice_in_dim(quantized, place_narrow * units, units, 1)

    if paired:
        half = col_width // 2
        forward = ladder_ring(chips)
        ring, spot = [], np.zeros(chips, np.int32)
        for i, chip in enumerate(forward):
            spot[chip] = i
            ring.append((2 * chip, 2 * forward[(i + 1) % chips]))
            ring.append((2 * chip + 1, 2 * forward[(i - 1) % chips] + 1))
        owners = np.zeros((wide, wide), np.int32)
        for w in range(wide):
            for k in range(chips):
                owners[w, k] = 2 * forward[(spot[w // 2] - (k if w % 2 == 0 else -k)) % chips] + w % 2
                owners[w, chips + k] = 2 * forward[(spot[w // 2] + (k if w % 2 == 0 else -k)) % chips] + 1 - w % 2
        back = np.argsort(owners, axis=1).astype(np.int32)
        order = lax.dynamic_index_in_dim(jnp.asarray(owners), place_wide, 0, keepdims=False)
        inverse_order = lax.dynamic_index_in_dim(jnp.asarray(back), place_wide, 0, keepdims=False)
        held = [
            jnp.concatenate([rot_half[:, at : at + half], cotangent[:, at : at + half]], axis=0)
            for at in (0, half)
        ]
        block_parts = []
        mine = [[h] for h in held]
        for k in range(chips - 1):
            for part in range(2):
                mine[part].append(lax.ppermute(mine[part][-1], "wide", ring))
        block_parts = [m + [other_core(b) for b in m] for m in mine]
        stacks = [jnp.stack([b[block_rows:] for b in part]) for part in block_parts]
        targets = jnp.concatenate(
            [jnp.take(s, inverse_order, axis=0).reshape(tokens, half) for s in stacks], axis=1
        )
        count = 8
        rows = units // count
        w_far = []
        for i in range(count):
            piece = down_weight[i * rows : (i + 1) * rows]
            if i >= 2:
                piece, w_far[i - 2] = lax.optimization_barrier((piece, w_far[i - 2]))
            w_far.append(other_narrow(piece))
    else:
        gathered = lax.all_gather(rot_half, "wide", axis=0, tiled=True)
        block_parts = [[gathered[i * block_rows : (i + 1) * block_rows] for i in range(wide)]]
        order = jnp.arange(wide, dtype=jnp.int32)
        targets = lax.all_gather(cotangent, "wide", axis=0, tiled=True)

    partial = jnp.dot(q_own, down_weight, preferred_element_type=jnp.float32)
    if paired:
        pieces = jnp.transpose(partial.reshape(tokens, chips, 2, block_rows), (1, 2, 0, 3))
        mixed_cols = sum_narrow(scatter_chips(pieces)).astype(jnp.bfloat16)
        near = exchange(jnp.broadcast_to(mixed_cols[None], (chips, tokens, block_rows)))
        beside = other_core(near)
        even = jnp.where(core == 0, near, beside)
        odd = jnp.where(core == 0, beside, near)
        u_full = jnp.transpose(jnp.stack([even, odd], axis=1), (2, 0, 1, 3)).reshape(tokens, width)
    else:
        mixed_cols = lax.psum_scatter(partial, "wide", scatter_dimension=1, tiled=True)
        mixed_cols = sum_narrow(mixed_cols).astype(jnp.bfloat16)
        u_full = lax.all_gather(mixed_cols, "wide", axis=1, tiled=True)

    scale = jnp.exp2(column_exps.astype(jnp.float32))[None, :]
    inverse = 1.0 / (LEVELS * scale)
    if paired:
        q_far = lax.dynamic_slice_in_dim(quantized, (1 - place_narrow) * units, units, 1)
        own, mix = panel_product(order, q_own, u_full, inverse, scale, [down_weight], block_parts, True)
        (far_part,) = panel_product(order, q_far, u_full, inverse, scale, w_far, block_parts, False)
        total = own + far_part
        pieces = total.reshape(chips, 2, tokens // wide, col_width)
        projected = scatter_chips(pieces)
    else:
        panel = lax.all_gather(down_weight, "narrow", axis=0, tiled=True)
        total, mix = panel_product(order, quantized, u_full, inverse, scale, [panel], block_parts, True)
        projected = lax.psum_scatter(total, "wide", scatter_dimension=0, tiled=True)

    across = (((1,), (1,)), ((), ()))
    p_part = lax.dot_general(targets, rot_half, across, preferred_element_type=jnp.float32)
    a_part = lax.dot_general(targets, mix.astype(jnp.bfloat16), across, preferred_element_type=jnp.float32)
    both = sum_narrow(jnp.concatenate([p_part, a_part], axis=1))
    p_cols, a_mat = both[:, :block_rows], both[:, block_rows:]
    b_mat = lax.dot_general(u_full, u_full, across, preferred_element_type=jnp.float32)
    mats = jnp.concatenate([a_mat, b_mat], axis=0)
    shifted = jnp.dot(mats.astype(jnp.bfloat16), targets, preferred_element_type=jnp.float32)
    v = 2.0 * targets.astype(jnp.float32) - step_size * shifted[:tokens]
    z = 2.0 * mix - step_size * shifted[tokens:]
    left = jnp.concatenate([mixed_cols, -p_cols.astype(jnp.bfloat16)], axis=0)
    right = jnp.concatenate([v, z], axis=0).astype(jnp.bfloat16)
    turned = lax.dot_general(left, right, (((0,), (0,)), ((), ())), preferred_element_type=jnp.float32)
    current = rotation - 0.5 * step_size * turned
    return projected.astype(jnp.bfloat16), math.sqrt(width) * current


def solution(mesh):
    in_specs = (
        P("wide", "narrow"),
        P(("wide", "narrow"), None),
        P("wide", "narrow"),
        P("wide", "narrow"),
        P("wide"),
        P("narrow"),
        P("narrow"),
        P(),
    )
    out_specs = (P("wide", "narrow"), P("wide", "narrow"))
    body = functools.partial(on_device, mesh.shape["wide"], mesh.shape["narrow"])
    return jax.shard_map(body, mesh=mesh, in_specs=in_specs, out_specs=out_specs, check_vma=False)
```
